32 devices in a mesh: fsdp: 2 (over x), context: 4 (over y, core), tensor: 4 (over z).
Axes of the slice: x: 2, y: 2, z: 4, core: 2. Of those that a mesh axis runs over, the one named last changes fastest.
Arguments:
- tokens: bfloat16 [2, 2048, 1024], P('fsdp', 'context'), may hold values from -6 to 6
- cotangent: bfloat16 [2, 2048, 1024], P('fsdp', 'context'), may hold values from -6 to 6
- lengths: int32 [2, 4], P('fsdp'), may hold values from 1 to 1024, 2048 in all within a row
- w_in: bfloat16 [3, 1024, 1024], P(None, 'fsdp', 'tensor'), may hold values from -0.1875 to 0.1875
- w_out: bfloat16 [1024, 1024], P('tensor', 'fsdp'), may hold values from -0.1875 to 0.1875
- w_gate_up: bfloat16 [2, 1024, 4608], P(None, 'fsdp', 'tensor'), may hold values from -0.1875 to 0.1875
- w_down: bfloat16 [4608, 1024], P('tensor', 'fsdp'), may hold values from -0.1875 to 0.1875
- norm_gains: bfloat16 [2, 1024], P(None, 'fsdp'), may hold values from 0.5 to 1.5
- conv_kernel: bfloat16 [3, 1024], P(None, 'tensor'), may hold values from -3 to 3
Outputs:
- block_out: float32 [2, 2048, 1024], P('fsdp', 'context')
- grad_tokens: float32 [2, 2048, 1024], P('fsdp', 'context')
- grad_w_in: float32 [3, 1024, 1024], P(None, 'fsdp', 'tensor')
- grad_w_out: float32 [1024, 1024], P('tensor', 'fsdp')
- grad_w_gate_up: float32 [2, 1024, 4608], P(None, 'fsdp', 'tensor')
- grad_w_down: float32 [4608, 1024], P('tensor', 'fsdp')
- grad_norm_gains: float32 [2, 1024], P(None, 'fsdp')
- grad_conv_kernel: float32 [3, 1024], P(None, 'tensor')
The draws below stay inside these ranges and needn't reach their ends.
Inputs may be any that keep to these rules, and one draw needn't show every extreme that they name: `lengths`: each row of 2048 tokens is a pack of 4 whole documents, in order; some document of every row has 1024 tokens.
All inputs are finite; a program needn't handle non-finite values.
Results may differ from the reference program's by a relative error of at most 0.0088.
Values may be sent and summed in bfloat16 or wider, within the bound.
No kernel may reach another device: no remote copies, remote signals or barrier semaphores. Data moves between devices by JAX's collectives and lax.ppermute only.
A program may use at most 128 MiB of HBM per device.

```python
import math
import jax
import jax.numpy as jnp
import numpy as np
from jax import lax

D = 1024
FF = 4608
TAPS = 3
DOCS = 4
SEQ = 2048
N_FSDP = 2


def block_levels(rng, dims, pieces, least, top_value):
    factor_of = 1.0
    for dim, blocks in pieces:
        steps = jax.random.uniform(jax.random.fold_in(jax.random.fold_in(rng, 6), dim), (blocks,), jnp.float32, least / len(pieces), top_value / len(pieces))
        factor_of = factor_of * jnp.repeat(jnp.exp(steps), dims[dim] // blocks).reshape((-1,) + (1,) * (len(dims) - 1 - dim))
    return factor_of


def split_up(count, total, limit, lean):
    loads = [(1 << 20) // math.isqrt(rank ** lean) + 1 for rank in range(2, count + 1)]
    spare, given = total - limit - (count - 1), [1] * (count - 1)
    while spare > 0:
        movable = [i for i in range(count - 1) if given[i] < limit]
        mass, remaining = sum([loads[i] for i in movable]), spare
        for i in movable:
            addition = min(limit - given[i], max(1, remaining * loads[i] // mass), spare)
            given[i] = given[i] + addition
            spare = spare - addition
    return np.array([limit] + given)


def ragged(rng, count, total, most, skew):
    if count == 2:
        one = jax.random.randint(rng, (), max(1, total - most), min(most, total - 1) + 1)
        return jnp.stack([one, total - one])
    sizes = jnp.asarray(split_up(count, total, most, skew), jnp.int32)
    twos = (count - 1) // 2
    source_of, sink = sizes[1:1 + 2 * twos:2], sizes[2:2 + 2 * twos:2]
    room = jnp.minimum(source_of - 1, most - sink)
    shifted = jax.random.randint(jax.random.fold_in(rng, 1), (twos,), 0, 1 << 20) % (room + 1)
    sizes = sizes.at[1:1 + 2 * twos:2].set(source_of - shifted).at[2:2 + 2 * twos:2].set(sink + shifted)
    return sizes[jax.random.permutation(jax.random.fold_in(rng, 2), count)]


def normal_values(rng, shape, spread, bound, pieces=(), kind=jnp.bfloat16):
    level = block_levels(rng, shape, pieces, -0.22, 0.18) if pieces else 1.0
    values = jax.random.normal(rng, shape, jnp.float32) * spread * level
    return jnp.minimum(jnp.maximum(values, -bound), bound).astype(kind)


def setup_inputs(seed: int = 0) -> dict:
    arg_keys = jax.random.split(jax.random.key(seed), 10)
    return {
        "tokens": normal_values(arg_keys[0], (N_FSDP, SEQ, D), 1.0, 6.0, ((0, 2), (1, 4))),
        "cotangent": normal_values(arg_keys[1], (N_FSDP, SEQ, D), 1.0, 6.0, ((0, 2), (1, 4))),
        "lengths": jax.vmap(lambda own: ragged(own, DOCS, SEQ, SEQ // 2, 2))(jax.random.split(arg_keys[2], N_FSDP)).reshape((N_FSDP, DOCS)).astype(jnp.int32),
        "w_in": normal_values(arg_keys[3], (3, D, D), D ** -0.5, 0.1875, ((1, 2), (2, 4))),
        "w_out": normal_values(arg_keys[4], (D, D), D ** -0.5, 0.1875, ((0, 4), (1, 2))),
        "w_gate_up": normal_values(arg_keys[5], (2, D, FF), D ** -0.5, 0.1875, ((1, 2), (2, 4))),
        "w_down": normal_values(arg_keys[6], (FF, D), (FF // 4) ** -0.5, 0.1875, ((0, 4), (1, 2))),
        "norm_gains": jnp.clip(1.0 + 0.1 * jax.random.normal(arg_keys[7], (2, D), jnp.float32), 0.5, 1.5).astype(jnp.bfloat16),
        "conv_kernel": normal_values(arg_keys[8], (TAPS, D), 0.6, 3.0, ((1, 4),)),
    }


norm_eps = 1e-05

def matmul_plain(matrix_one, matrix_two):
    return jnp.dot(matrix_one, matrix_two, preferred_element_type=jnp.float32)

def matmul_right(matrix_one, matrix_two):
    return lax.dot_general(matrix_one, matrix_two, (((1,), (1,)), ((), ())), preferred_element_type=jnp.float32)

def matmul_left(matrix_one, matrix_two):
    return lax.dot_general(matrix_one, matrix_two, (((0,), (0,)), ((), ())), preferred_element_type=jnp.float32)

def norm_forward(values):
    inv_root = lax.rsqrt(lax.optimization_barrier(jnp.mean(values * values, axis=-1, keepdims=True)) + norm_eps)
    return (values * inv_root, inv_root)

def norm_backward(normed, inv_root, gain_row, grad_out):
    grad_normed = grad_out * gain_row
    inner_mean = lax.optimization_barrier(jnp.mean(grad_normed * normed, axis=-1, keepdims=True))
    return (inv_root * (grad_normed - normed * inner_mean), lax.optimization_barrier(jnp.sum(grad_out * normed, axis=0)))

def keep_masks(position, lengths_row):
    starts = jnp.cumsum(lengths_row) - lengths_row
    doc_start = lax.optimization_barrier(jnp.max(jnp.where(starts[None, :] <= position[:, None], starts[None, :], 0), axis=1))
    keep_one = (position - 1 >= doc_start).astype(jnp.float32)[:, None]
    keep_two = (position - 2 >= doc_start).astype(jnp.float32)[:, None]
    return (keep_one, keep_two)

def one_row(row_tokens, row_cotangent, lengths_row, w_in, w_out, w_gate_up, w_down, norm_gains, conv_kernel):
    row_count = row_tokens.shape[0]
    position = jnp.arange(row_count, dtype=jnp.int32)
    keep_one, keep_two = keep_masks(position, lengths_row)
    inputs = row_tokens.astype(jnp.float32)
    gain_first = norm_gains[0].astype(jnp.float32)
    gain_second = norm_gains[1].astype(jnp.float32)
    kernel_taps = conv_kernel.astype(jnp.float32)
    width = inputs.shape[1]
    normed_one, root_one = norm_forward(inputs)
    hidden_one = (normed_one * gain_first).astype(jnp.bfloat16)
    b_part = matmul_plain(hidden_one, w_in[0])
    c_part = matmul_plain(hidden_one, w_in[1])
    x_part = matmul_plain(hidden_one, w_in[2])
    mixed = b_part * x_part
    back_one = jnp.concatenate([jnp.zeros((1, width), jnp.float32), mixed[:-1]], axis=0) * keep_one
    back_two = jnp.concatenate([jnp.zeros((2, width), jnp.float32), mixed[:-2]], axis=0) * keep_two
    conv_value = kernel_taps[2] * mixed + kernel_taps[1] * back_one + kernel_taps[0] * back_two
    gated = (c_part * conv_value).astype(jnp.bfloat16)
    first_sum = inputs + matmul_plain(gated, w_out)
    normed_two, root_two = norm_forward(first_sum)
    hidden_two = (normed_two * gain_second).astype(jnp.bfloat16)
    gate_value = matmul_plain(hidden_two, w_gate_up[0])
    up_value = matmul_plain(hidden_two, w_gate_up[1])
    sigmoid_gate = jax.nn.sigmoid(gate_value)
    silu_gate = gate_value * sigmoid_gate
    act_value = (silu_gate * up_value).astype(jnp.bfloat16)
    output_rows = first_sum + matmul_plain(act_value, w_down)
    grad_act = matmul_right(row_cotangent, w_down)
    grad_gate = (grad_act * up_value * sigmoid_gate * (1.0 + gate_value * (1.0 - sigmoid_gate))).astype(jnp.bfloat16)
    grad_up = (grad_act * silu_gate).astype(jnp.bfloat16)
    grad_h2 = matmul_right(grad_gate, w_gate_up[0]) + matmul_right(grad_up, w_gate_up[1])
    back_second, grad_gain_two = norm_backward(normed_two, root_two, gain_second, grad_h2)
    grad_first = row_cotangent.astype(jnp.float32) + back_second
    grad_first_b = grad_first.astype(jnp.bfloat16)
    grad_gated = matmul_right(grad_first_b, w_out)
    grad_conv = grad_gated * c_part
    ahead_one = jnp.concatenate([grad_conv[1:] * keep_one[1:], jnp.zeros((1, width), jnp.float32)], axis=0)
    ahead_two = jnp.concatenate([grad_conv[2:] * keep_two[2:], jnp.zeros((2, width), jnp.float32)], axis=0)
    grad_mixed = kernel_taps[2] * grad_conv + kernel_taps[1] * ahead_one + kernel_taps[0] * ahead_two
    grad_kernel = jnp.stack([lax.optimization_barrier(jnp.sum(grad_conv * back_two, axis=0)), lax.optimization_barrier(jnp.sum(grad_conv * back_one, axis=0)), lax.optimization_barrier(jnp.sum(grad_conv * mixed, axis=0))])
    grad_b = (grad_mixed * x_part).astype(jnp.bfloat16)
    grad_c = (grad_gated * conv_value).astype(jnp.bfloat16)
    grad_x = (grad_mixed * b_part).astype(jnp.bfloat16)
    grad_h1 = matmul_right(grad_b, w_in[0]) + matmul_right(grad_c, w_in[1]) + matmul_right(grad_x, w_in[2])
    back_first, grad_gain_one = norm_backward(normed_one, root_one, gain_first, grad_h1)
    grad_inputs = grad_first + back_first
    grads = (jnp.stack([matmul_left(hidden_one, grad_b), matmul_left(hidden_one, grad_c), matmul_left(hidden_one, grad_x)]), matmul_left(gated, grad_first_b), jnp.stack([matmul_left(hidden_two, grad_gate), matmul_left(hidden_two, grad_up)]), matmul_left(act_value, row_cotangent), jnp.stack([grad_gain_one, grad_gain_two]), grad_kernel)
    return (output_rows, grad_inputs, grads)

def reference(tokens, cotangent, lengths, w_in, w_out, w_gate_up, w_down, norm_gains, conv_kernel):

    def row_step(running, row_item):
        row_tokens, row_cotangent, lengths_row = row_item
        output_rows, grad_inputs, grads = one_row(row_tokens, row_cotangent, lengths_row, w_in, w_out, w_gate_up, w_down, norm_gains, conv_kernel)
        return (jax.tree.map(lambda total, term: total + term, running, grads), (output_rows, grad_inputs))
    initial = (jnp.zeros((3, D, D), jnp.float32), jnp.zeros((D, D), jnp.float32), jnp.zeros((2, D, FF), jnp.float32), jnp.zeros((FF, D), jnp.float32), jnp.zeros((2, D), jnp.float32), jnp.zeros((TAPS, D), jnp.float32))
    totals, stacked = lax.scan(row_step, initial, (tokens, cotangent, lengths))
    return (stacked[0], stacked[1], totals[0], totals[1], totals[2], totals[3], totals[4], totals[5])
```

```python
import jax
import jax.numpy as jnp
from jax import lax
from jax.sharding import PartitionSpec as P

norm_eps = 1e-05
f32 = jnp.float32
bf16 = jnp.bfloat16


def swap(block, axis, mask):
    return lax.ppermute(block, axis, [(i, i ^ mask) for i in range(lax.axis_size(axis))])


def shifted(block, axis, distance):
    devices = range(lax.axis_size(axis))
    return lax.ppermute(block, axis, [(i - distance, i) for i in devices if i - distance in devices])


def pick(blocks, index, dim=0):
    return lax.dynamic_index_in_dim(blocks, index, dim, keepdims=False)


def matmul_plain(a, b):
    return jnp.dot(a, b, preferred_element_type=f32)


def matmul_right(a, b):
    return lax.dot_general(a, b, (((1,), (1,)), ((), ())), preferred_element_type=f32)


def matmul_left(a, b):
    return lax.dot_general(a, b, (((0,), (0,)), ((), ())), preferred_element_type=f32)


def gather_shards(shard, dim, cut):
    me, core = lax.axis_index("fsdp"), lax.axis_index("context") % 2
    size = shard.shape[dim]
    half = shard.shape[cut] // 2
    mine = lax.dynamic_slice_in_dim(shard, core * half, half, cut)
    shape = list(shard.shape)
    shape[dim] = size * lax.axis_size("fsdp")

    def put(full, piece, owner, part):
        start = [0] * shard.ndim
        start[dim] = owner * size
        start[cut] = start[cut] + part * half
        return lax.dynamic_update_slice(full, piece, start)

    full = put(jnp.zeros(shape, shard.dtype), shard, me, 0)
    for mask in range(1, lax.axis_size("fsdp")):
        first = swap(mine, "fsdp", mask)
        second = swap(first, "context", 1)
        full = put(full, first, me ^ mask, core)
        full = put(full, second, me ^ mask, 1 - core)
    return full


def tensor_scatter(partial):
    count, me = lax.axis_size("tensor"), lax.axis_index("tensor")
    blocks = partial.reshape(count, partial.shape[0] // count, partial.shape[1])
    total = pick(blocks, me).astype(f32)
    for mask in range(1, count):
        total = total + swap(pick(blocks, me ^ mask), "tensor", mask).astype(f32)
    return total


def tensor_gather(rows):
    count, me = lax.axis_size("tensor"), lax.axis_index("tensor")
    full = jnp.zeros((count,) + rows.shape, rows.dtype)
    full = lax.dynamic_update_index_in_dim(full, rows, me, 0)
    for mask in range(1, count):
        full = lax.dynamic_update_index_in_dim(full, swap(rows, "tensor", mask), me ^ mask, 0)
    return full.reshape(count * rows.shape[0], rows.shape[1])


def reduce_shards(partial, dim, cut):
    fs, ctx = lax.axis_index("fsdp"), lax.axis_index("context")
    n_fs, n_rest = lax.axis_size("fsdp"), lax.axis_size("context") // 2
    core, rest = ctx % 2, ctx // 2

    def part(value, axis, count, index):
        size = value.shape[axis] // count
        return lax.dynamic_slice_in_dim(value, index * size, size, axis)

    def fold(value, axis, count, index, name, scale):
        total = part(value, axis, count, index).astype(f32)
        for mask in range(1, count):
            piece = part(value, axis, count, index ^ mask).astype(bf16)
            total = total + swap(piece, name, mask * scale).astype(f32)
        return total

    def spread(piece, axis, count, index, name, scale):
        shape = list(piece.shape)
        shape[axis] *= count
        full = jnp.zeros(shape, piece.dtype)
        size = piece.shape[axis]
        full = lax.dynamic_update_slice_in_dim(full, piece, index * size, axis)
        for mask in range(1, count):
            full = lax.dynamic_update_slice_in_dim(
                full, swap(piece, name, mask * scale), (index ^ mask) * size, axis
            )
        return full

    if dim == cut:
        lead, tail = partial.shape[:dim], partial.shape[dim + 1 :]
        size = partial.shape[dim] // n_fs
        wide = partial.reshape(lead + (n_fs, size) + tail)
        wide = fold(wide, dim + 1, 2, core, "context", 1)
        value = fold(wide, dim, n_fs, fs, "fsdp", 1)
        value = value.reshape(lead + (size // 2,) + tail)
    else:
        value = fold(partial, cut, 2, core, "context", 1)
        value = fold(value, dim, n_fs, fs, "fsdp", 1)
    value = fold(value, cut, n_rest, rest, "context", 2).astype(bf16)
    value = spread(value, cut, n_rest, rest, "context", 2)
    return spread(value, cut, 2, core, "context", 1).astype(f32)


def sum_over(value, axes):
    for axis in axes:
        parts = [swap(value, axis, mask) for mask in range(1, lax.axis_size(axis))]
        count, me = lax.axis_size(axis), lax.axis_index(axis)
        table = jnp.zeros((count,) + value.shape, value.dtype)
        table = lax.dynamic_update_index_in_dim(table, value, me, 0)
        for mask in range(1, count):
            table = lax.dynamic_update_index_in_dim(table, parts[mask - 1], me ^ mask, 0)
        value = jnp.sum(table, axis=0)
    return value


def norm_forward(values):
    inv_root = lax.rsqrt(jnp.mean(values * values, axis=-1, keepdims=True) + norm_eps)
    return (values * inv_root, inv_root)


def norm_backward(normed, inv_root, gain_row, grad_out):
    grad_normed = grad_out * gain_row
    inner_mean = jnp.mean(grad_normed * normed, axis=-1, keepdims=True)
    return (inv_root * (grad_normed - normed * inner_mean), jnp.sum(grad_out * normed, axis=0))


def keep_masks(position, lengths_row):
    starts = jnp.cumsum(lengths_row) - lengths_row
    doc_start = jnp.max(jnp.where(starts[None, :] <= position[:, None], starts[None, :], 0), axis=1)
    keep_one = (position - 1 >= doc_start).astype(f32)[:, None]
    keep_two = (position - 2 >= doc_start).astype(f32)[:, None]
    return (keep_one, keep_two)


halo = 16


def local(tokens, cotangent, lengths, w_in, w_out, w_gate_up, w_down, norm_gains, conv_kernel):
    block_rows = tokens.shape[1]
    z = lax.axis_index("tensor")
    share = block_rows // lax.axis_size("tensor")
    position = lax.axis_index("context") * block_rows + jnp.arange(block_rows + 2, dtype=jnp.int32)
    keep_one_ext, keep_two_ext = keep_masks(position, lengths[0])
    keep_one = keep_one_ext[:block_rows]
    keep_two = keep_two_ext[:block_rows]

    own_tokens = tokens[0]
    cot_rows = cotangent[0]
    previous = shifted(own_tokens[-halo:], "context", 1)
    gains_t = gather_shards(norm_gains, 1, 1)
    full_in = gather_shards(w_in, 1, 1)
    full_out = gather_shards(w_out, 1, 0)
    full_gate_up = gather_shards(w_gate_up, 1, 1)
    full_down = gather_shards(w_down, 1, 0)

    gain_first = gains_t[0].astype(f32)
    gain_second = gains_t[1].astype(f32)
    taps = conv_kernel.astype(f32)

    inputs = jnp.concatenate([previous, own_tokens], axis=0).astype(f32)
    normed_ext, _ = norm_forward(inputs)
    hidden_ext = (normed_ext * gain_first).astype(bf16)
    hidden_one = hidden_ext[halo:]
    b_ext = matmul_plain(hidden_ext, full_in[0])
    x_ext = matmul_plain(hidden_ext, full_in[2])
    c_part = matmul_plain(hidden_one, full_in[1])
    b_part, x_part = b_ext[halo:], x_ext[halo:]
    mixed_ext = b_ext * x_ext
    mixed = mixed_ext[halo:]
    back_one = mixed_ext[halo - 1 : -1] * keep_one
    back_two = mixed_ext[halo - 2 : -2] * keep_two
    conv_value = taps[2] * mixed + taps[1] * back_one + taps[0] * back_two
    gated = (c_part * conv_value).astype(bf16)

    my_tokens = lax.dynamic_slice_in_dim(own_tokens, z * share, share, 0).astype(f32)
    my_cot = lax.dynamic_slice_in_dim(cot_rows, z * share, share, 0).astype(f32)
    first_sum = my_tokens + tensor_scatter(matmul_plain(gated, full_out).astype(bf16))
    normed_two, root_two = norm_forward(first_sum)
    hidden_two = tensor_gather((normed_two * gain_second).astype(bf16))

    gate_value = matmul_plain(hidden_two, full_gate_up[0])
    up_value = matmul_plain(hidden_two, full_gate_up[1])
    sigmoid_gate = jax.nn.sigmoid(gate_value)
    silu_gate = gate_value * sigmoid_gate
    act_value = (silu_gate * up_value).astype(bf16)
    grad_act = matmul_right(cot_rows, full_down)
    grad_gate = (
        grad_act * up_value * sigmoid_gate * (1.0 + gate_value * (1.0 - sigmoid_gate))
    ).astype(bf16)
    grad_up = (grad_act * silu_gate).astype(bf16)
    grad_h2 = tensor_scatter(
        (
            matmul_right(grad_gate, full_gate_up[0]) + matmul_right(grad_up, full_gate_up[1])
        ).astype(bf16)
    )
    down_rows = tensor_scatter(matmul_plain(act_value, full_down).astype(bf16))
    output_rows = tensor_gather((first_sum + down_rows).astype(bf16)).astype(f32)

    back_second, grad_gain_two = norm_backward(normed_two, root_two, gain_second, grad_h2)
    grad_first = my_cot + back_second
    grad_first_b = tensor_gather(grad_first.astype(bf16))
    grad_gated = matmul_right(grad_first_b, full_out)
    grad_conv = grad_gated * c_part
    next_rows = shifted(grad_conv[:2], "context", -1)
    ahead = jnp.concatenate([grad_conv, next_rows], axis=0)
    ahead_one = ahead[1 : block_rows + 1] * keep_one_ext[1 : block_rows + 1]
    ahead_two = ahead[2:] * keep_two_ext[2:]
    grad_mixed = taps[2] * grad_conv + taps[1] * ahead_one + taps[0] * ahead_two
    grad_kernel = jnp.stack(
        [
            jnp.sum(grad_conv * back_two, axis=0),
            jnp.sum(grad_conv * back_one, axis=0),
            jnp.sum(grad_conv * mixed, axis=0),
        ]
    )
    grad_b = (grad_mixed * x_part).astype(bf16)
    grad_c = (grad_gated * conv_value).astype(bf16)
    grad_x = (grad_mixed * b_part).astype(bf16)
    grad_h1 = tensor_scatter(
        (
            matmul_right(grad_b, full_in[0])
            + matmul_right(grad_c, full_in[1])
            + matmul_right(grad_x, full_in[2])
        ).astype(bf16)
    )
    normed_one, root_one = norm_forward(my_tokens)
    back_first, grad_gain_one = norm_backward(normed_one, root_one, gain_first, grad_h1)
    grad_inputs = tensor_gather((grad_first + back_first).astype(bf16)).astype(f32)

    gate_up_total = reduce_shards(
        jnp.stack([matmul_left(hidden_two, grad_gate), matmul_left(hidden_two, grad_up)]), 1, 1
    )
    down_total = reduce_shards(matmul_left(act_value, cot_rows), 1, 0)
    out_total = reduce_shards(matmul_left(gated, grad_first_b), 1, 0)
    in_total = reduce_shards(
        jnp.stack(
            [
                matmul_left(hidden_one, grad_b),
                matmul_left(hidden_one, grad_c),
                matmul_left(hidden_one, grad_x),
            ]
        ),
        1,
        1,
    )
    kernel_total = sum_over(grad_kernel, ("fsdp", "context"))
    gains_total = sum_over(
        jnp.stack([grad_gain_one, grad_gain_two]), ("tensor", "context", "fsdp")
    )
    gain_width = norm_gains.shape[1]
    gains_total = lax.dynamic_slice_in_dim(
        gains_total, lax.axis_index("fsdp") * gain_width, gain_width, 1
    )
    return (
        output_rows[None],
        grad_inputs[None],
        in_total,
        out_total,
        gate_up_total,
        down_total,
        gains_total,
        kernel_total,
    )


def solution(mesh):
    placed = (
        P("fsdp", "context", None),
        P("fsdp", "context", None),
        P("fsdp", None),
        P(None, "fsdp", "tensor"),
        P("tensor", "fsdp"),
        P(None, "fsdp", "tensor"),
        P("tensor", "fsdp"),
        P(None, "fsdp"),
        P(None, "tensor"),
    )
    return jax.shard_map(
        local,
        mesh=mesh,
        in_specs=placed,
        out_specs=(
            P("fsdp", "context", None),
            P("fsdp", "context", None),
            P(None, "fsdp", "tensor"),
            P("tensor", "fsdp"),
            P(None, "fsdp", "tensor"),
            P("tensor", "fsdp"),
            P(None, "fsdp"),
            P(None, "tensor"),
        ),
        check_vma=False,
    )
```

```python
import jax
import jax.numpy as jnp
from jax import lax
from jax.experimental import pallas as pl
from jax.experimental.pallas import tpu as pltpu
from jax.sharding import PartitionSpec as P


norm_eps = 1e-05
f32 = jnp.float32
bf16 = jnp.bfloat16
halo = 16


def swap(block, axis, mask):
    return lax.ppermute(block, axis, [(i, i ^ mask) for i in range(lax.axis_size(axis))])


def after(value, *deps):
    return lax.optimization_barrier((value,) + deps)[0]


def shifted(block, axis, distance):
    devices = range(lax.axis_size(axis))
    return lax.ppermute(block, axis, [(i - distance, i) for i in devices if i - distance in devices])


def dot(a, b):
    return jnp.dot(a, b, preferred_element_type=f32)


def dot_right(a, b):
    return lax.dot_general(a, b, (((1,), (1,)), ((), ())), preferred_element_type=f32)


def dot_left(a, b):
    return lax.dot_general(a, b, (((0,), (0,)), ((), ())), preferred_element_type=f32)


def fetch_shards(shard, cut):
    core = lax.axis_index("context") % 2
    half = shard.shape[cut] // 2
    mine = lax.dynamic_slice_in_dim(shard, core * half, half, cut)
    return [swap(mine, "fsdp", mask) for mask in range(1, lax.axis_size("fsdp"))]


def swap_cores(pieces):
    return [swap(piece, "context", 1) for piece in pieces]


def tensor_swap(blocks):
    return [swap(blocks[mask], "tensor", mask) for mask in range(1, len(blocks))]


def call(body, outs, ins, scratch=(), any_ins=(), flops=0):
    size = lambda a: a.size * a.dtype.itemsize
    kernel = pl.pallas_call(
        body,
        out_shape=[jax.ShapeDtypeStruct(s, d) for s, d in outs],
        in_specs=[
            pl.BlockSpec(memory_space=pltpu.SMEM if a.dtype == jnp.int32 else pltpu.VMEM)
            for a in ins
        ]
        + [pl.BlockSpec(memory_space=pl.ANY) for _ in any_ins],
        out_specs=[pl.BlockSpec(memory_space=pltpu.VMEM) for _ in outs],
        scratch_shapes=list(scratch),
        compiler_params=pltpu.CompilerParams(vmem_limit_bytes=56 << 20),
        cost_estimate=pl.CostEstimate(
            flops=flops,
            transcendentals=0,
            bytes_accessed=sum(size(a) for a in list(ins) + list(any_ins)),
        ),
    )
    return kernel(*ins, *any_ins)


def mult(value, by):
    return pl.multiple_of(value, by)


def shard_places(shape, dim, cut, n_fs):
    me, core = lax.axis_index("fsdp"), lax.axis_index("context") % 2
    size, half = shape[dim], shape[cut] // 2

    def place(owner, part):
        index = []
        for axis, extent in enumerate(shape):
            start, length, unit = 0, extent, extent
            if axis == dim:
                start, unit = owner * size, size
            if axis == cut and part is not None:
                start, length, unit = start + part * half, half, half
            index.append(slice(None) if isinstance(start, int) else pl.ds(mult(start, unit), length))
        return tuple(index)

    own = [place(me, None)]
    firsts = [place(me ^ mask, core) for mask in range(1, n_fs)]
    seconds = [place(me ^ mask, 1 - core) for mask in range(1, n_fs)]
    return own + firsts + seconds


class Assembled:
    def __init__(self, pieces, dim, cut, n_fs):
        self.pieces, self.dim, self.cut, self.n_fs = pieces, dim, cut, n_fs
        self.local = pieces[0].shape
        self.shape = tuple(
            s * n_fs if axis == dim else s for axis, s in enumerate(self.local)
        )
        self.count = len(pieces)

    def scratch(self):
        return [pltpu.VMEM(self.shape, bf16), pltpu.SemaphoreType.DMA((self.count,))]

    def copies(self, refs, whole, sems):
        places = shard_places(self.local, self.dim, self.cut, self.n_fs)
        return [
            pltpu.make_async_copy(ref, whole.at[place], sems.at[i])
            for i, (ref, place) in enumerate(zip(refs, places))
        ]


def row_rms(v):
    return lax.rsqrt(jnp.mean(v * v, axis=-1, keepdims=True) + norm_eps)


def keeps(lengths_ref, first, shape):
    position = first + lax.broadcasted_iota(jnp.int32, shape, 0)
    start = jnp.int32(0)
    one = jnp.ones(shape, jnp.bool_)
    two = jnp.ones(shape, jnp.bool_)
    for doc in range(lengths_ref.shape[1]):
        one = one & (position != start)
        two = two & (position != start + 1)
        start = start + lengths_ref[0, doc]
    two = two & one
    return one.astype(f32), two.astype(f32)


def split_rows(ref, outs, z):
    rows = outs[0].shape[0]
    for mask, out in enumerate(outs):
        out[...] = ref[pl.ds(mult((z ^ mask) * rows, rows), rows), :]


def join_rows(ref, blocks, z):
    rows = blocks[0].shape[0]
    for mask, block in enumerate(blocks):
        ref[pl.ds(mult((z ^ mask) * rows, rows), rows), :] = block[...].astype(ref.dtype)


def mixer_forward(lengths, tokens, before, behind, gains, taps, w_in, w_out, nz):
    rows, width = tokens.shape
    chan = w_in.local[2]
    ext = rows + 2 * halo
    share = rows // nz

    def body(*refs):
        len_ref, tok, prev, nxt, gain, tap = refs[:6]
        refs = refs[6:]
        in_refs, refs = refs[: w_in.count], refs[w_in.count :]
        out_refs, refs = refs[: w_out.count], refs[w_out.count :]
        parts, refs = refs[:nz], refs[nz:]
        h_out, b_out, c_out, x_out, gated_out = refs[:5]
        win, sem_in, wout, sem_out, hid, mixed, whole = refs[5:]
        z, ctx = lax.axis_index("tensor"), lax.axis_index("context")
        copy_in = w_in.copies(in_refs, win, sem_in)
        copy_out = w_out.copies(out_refs, wout, sem_out)
        for copy in copy_in + copy_out:
            copy.start()
        g = gain[...].astype(f32)

        def hidden(v):
            v = v.astype(f32)
            return (v * row_rms(v) * g).astype(bf16)

        hid[:halo, :] = hidden(prev[...])
        hid[halo + rows :, :] = hidden(nxt[...])
        body_rows = hidden(tok[...])
        hid[halo : halo + rows, :] = body_rows
        h_out[...] = body_rows
        for copy in copy_in:
            copy.wait()
        h = hid[...]
        b = dot(h, win[0])
        x = dot(h, win[2])
        c = dot(h, win[1])
        b_out[...] = b
        x_out[...] = x
        c_out[...] = c
        mixed[...] = b * x
        one, two = keeps(len_ref, ctx * rows, (rows, chan))
        t = tap[...].astype(f32)
        conv = (
            t[2:3] * mixed[halo : halo + rows, :]
            + t[1:2] * (mixed[halo - 1 : halo + rows - 1, :] * one)
            + t[0:1] * (mixed[halo - 2 : halo + rows - 2, :] * two)
        )
        gated = (c[halo : halo + rows] * conv).astype(bf16)
        gated_out[...] = gated
        for copy in copy_out:
            copy.wait()
        whole[...] = dot(gated, wout[...]).astype(bf16)
        split_rows(whole, parts, z)

    return call(
        body,
        [((share, width), bf16)] * nz
        + [((rows, width), bf16)]
        + [((ext, chan), f32)] * 3
        + [((rows, chan), bf16)],
        [lengths, tokens, before, behind, gains, taps],
        w_in.scratch()
        + w_out.scratch()
        + [
            pltpu.VMEM((ext, width), bf16),
            pltpu.VMEM((ext, chan), f32),
            pltpu.VMEM((rows, width), bf16),
        ],
        w_in.pieces + w_out.pieces,
        flops=8 * rows * width * chan,
    )


def first_norm(own, received, tokens, gains):
    share, width = own.shape

    def body(*refs):
        own_ref = refs[0]
        others, refs = refs[1 : 1 + len(received)], refs[1 + len(received) :]
        tok, gain, x1_out, h2_out = refs
        z = lax.axis_index("tensor")
        total = tok[pl.ds(mult(z * share, share), share), :].astype(f32)
        total = total + own_ref[...].astype(f32)
        for other in others:
            total = total + other[...].astype(f32)
        x1_out[...] = total
        h2_out[...] = (total * row_rms(total) * gain[...].astype(f32)).astype(bf16)

    return call(
        body, [((share, width), f32), ((share, width), bf16)], [own, *received, tokens, gains]
    )


def feed_forward(own, received, cot, w_gate_up, w_down, nz):
    rows, width = cot.shape
    share = rows // nz
    hidden = w_gate_up.shape[2]
    tile = next(t for t in (384, 256, 128, hidden) if hidden % t == 0)

    def body(*refs):
        blocks, refs = refs[:nz], refs[nz:]
        cot_ref, refs = refs[0], refs[1:]
        gu_refs, refs = refs[: w_gate_up.count], refs[w_gate_up.count :]
        d_refs, refs = refs[: w_down.count], refs[w_down.count :]
        parts, refs = refs[:nz], refs[nz:]
        h2_out, gg_out, gu_out, act_out = refs[:4]
        wgu, sem_gu, wd, sem_d, acc = refs[4:]
        z = lax.axis_index("tensor")
        copy_d = w_down.copies(d_refs, wd, sem_d)
        copy_gu = w_gate_up.copies(gu_refs, wgu, sem_gu)
        for copy in copy_d + copy_gu:
            copy.start()
        join_rows(h2_out, blocks, z)
        acc[...] = jnp.zeros_like(acc)
        for copy in copy_d + copy_gu:
            copy.wait()

        @pl.loop(0, hidden // tile)
        def _(step):
            columns = pl.ds(mult(step * tile, tile), tile)
            h2 = h2_out[...]
            wg, wu = wgu[0, :, columns], wgu[1, :, columns]
            grad_act = dot_right(cot_ref[...], wd[columns, :])
            gate = dot(h2, wg)
            up = dot(h2, wu)
            sig = jax.nn.sigmoid(gate)
            silu = gate * sig
            act_out[:, columns] = (silu * up).astype(bf16)
            gg = (grad_act * up * sig * (1.0 + gate * (1.0 - sig))).astype(bf16)
            gu = (grad_act * silu).astype(bf16)
            gg_out[:, columns] = gg
            gu_out[:, columns] = gu
            acc[...] += dot_right(gg, wg) + dot_right(gu, wu)

        for mask, part in enumerate(parts):
            part[...] = acc[pl.ds(mult((z ^ mask) * share, share), share), :].astype(bf16)

    return call(
        body,
        [((share, width), bf16)] * nz + [((rows, width), bf16)] + [((rows, hidden), bf16)] * 3,
        [own, *received, cot],
        w_gate_up.scratch() + w_down.scratch() + [pltpu.VMEM((rows, width), f32)],
        w_gate_up.pieces + w_down.pieces,
        flops=10 * rows * width * hidden,
    )


def down_product(act, w_down, nz):
    rows, hidden = act.shape
    width = w_down.shape[1]
    share = rows // nz

    def body(*refs):
        act_ref, refs = refs[0], refs[1:]
        d_refs, refs = refs[: w_down.count], refs[w_down.count :]
        parts, (wd, sem_d, whole) = refs[:nz], refs[nz:]
        z = lax.axis_index("tensor")
        copies = w_down.copies(d_refs, wd, sem_d)
        for copy in copies:
            copy.start()
        for copy in copies:
            copy.wait()
        whole[...] = dot(act_ref[...], wd[...]).astype(bf16)
        split_rows(whole, parts, z)

    return call(
        body,
        [((share, width), bf16)] * nz,
        [act],
        w_down.scratch() + [pltpu.VMEM((rows, width), bf16)],
        w_down.pieces,
        flops=2 * rows * width * hidden,
    )


def norm_back(own, received, values, gains, base):
    share, width = own.shape
    n = len(received)
    whole_values, whole_base = values.shape[0] != share, base.shape[0] != share

    def body(*refs):
        own_ref, others, refs = refs[0], refs[1 : 1 + n], refs[1 + n :]
        val, gain, add, out, out_b, grad_gain = refs
        z = lax.axis_index("tensor")
        mine = pl.ds(mult(z * share, share), share)
        e = own_ref[...].astype(f32)
        for other in others:
            e = e + other[...].astype(f32)
        v = (val[mine, :] if whole_values else val[...]).astype(f32)
        start = (add[mine, :] if whole_base else add[...]).astype(f32)
        r = row_rms(v)
        normed = v * r
        eg = e * gain[...].astype(f32)
        inner = jnp.mean(eg * normed, axis=-1, keepdims=True)
        total = start + r * (eg - normed * inner)
        out[...] = total
        out_b[...] = total.astype(bf16)
        grad_gain[...] = jnp.sum(e * normed, axis=0, keepdims=True)

    return call(
        body,
        [((share, width), f32), ((share, width), bf16), ((1, width), f32)],
        [own, *received, values, gains, base],
    )


def mixer_backward(lengths, own, received, halos, b_ext, c_ext, x_ext, taps, w_in, w_out, nz):
    share, width = own.shape
    rows = share * nz
    chan = w_in.local[2]
    ext = rows + halo

    def body(*refs):
        len_ref, refs = refs[0], refs[1:]
        blocks, refs = refs[:nz], refs[nz:]
        ahead, refs = refs[:nz], refs[nz:]
        b_ref, c_ref, x_ref, tap = refs[:4]
        refs = refs[4:]
        in_refs, refs = refs[: w_in.count], refs[w_in.count :]
        out_refs, refs = refs[: w_out.count], refs[w_out.count :]
        parts, refs = refs[:nz], refs[nz:]
        gx_out, gb_out, gc_out, gxx_out, tap_out = refs[:5]
        win, sem_in, wout, sem_out, gx, keep1, keep2, mixed = refs[5:]
        z, ctx = lax.axis_index("tensor"), lax.axis_index("context")
        copy_out = w_out.copies(out_refs, wout, sem_out)
        copy_in = w_in.copies(in_refs, win, sem_in)
        for copy in copy_out + copy_in:
            copy.start()
        join_rows(gx, blocks, z)
        gx_out[...] = gx[:rows, :]
        tail = ahead[0][...]
        for mask in range(1, nz):
            tail = jnp.where(z == mask, ahead[mask][...], tail)
        gx[rows:, :] = tail
        one, two = keeps(len_ref, ctx * rows, (ext, chan))
        t = tap[...].astype(f32)
        mixed[...] = b_ref[: halo + rows, :] * x_ref[: halo + rows, :]
        here = mixed[halo:, :]
        back1 = mixed[halo - 1 : halo + rows - 1, :] * one[:rows]
        back2 = mixed[halo - 2 : halo + rows - 2, :] * two[:rows]
        conv = t[2:3] * here + t[1:2] * back1 + t[0:1] * back2
        for copy in copy_out:
            copy.wait()
        grad_gated = dot_right(gx[...], wout[...])
        grad_conv_ext = grad_gated * c_ref[halo:, :]
        grad_conv = grad_conv_ext[:rows]
        keep1[...] = grad_conv_ext * one
        keep2[...] = grad_conv_ext * two
        grad_mixed = (
            t[2:3] * grad_conv + t[1:2] * keep1[1 : rows + 1, :] + t[0:1] * keep2[2 : rows + 2, :]
        )
        gb = (grad_mixed * x_ref[halo : halo + rows, :]).astype(bf16)
        gc = (grad_gated[:rows] * conv).astype(bf16)
        gxx = (grad_mixed * b_ref[halo : halo + rows, :]).astype(bf16)
        gb_out[...] = gb
        gc_out[...] = gc
        gxx_out[...] = gxx
        tap_out[0:1, :] = jnp.sum(grad_conv * back2, axis=0, keepdims=True)
        tap_out[1:2, :] = jnp.sum(grad_conv * back1, axis=0, keepdims=True)
        tap_out[2:3, :] = jnp.sum(grad_conv * here, axis=0, keepdims=True)
        for copy in copy_in:
            copy.wait()
        total = dot_right(gb, win[0]) + dot_right(gc, win[1]) + dot_right(gxx, win[2])
        gx[:rows, :] = total.astype(bf16)
        split_rows(gx, parts, z)

    return call(
        body,
        [((share, width), bf16)] * nz
        + [((rows, width), bf16)]
        + [((rows, chan), bf16)] * 3
        + [((3, chan), f32)],
        [lengths, own, *received, *halos, b_ext, c_ext, x_ext, taps],
        w_in.scratch()
        + w_out.scratch()
        + [
            pltpu.VMEM((ext, width), bf16),
            pltpu.VMEM((ext, chan), f32),
            pltpu.VMEM((ext, chan), f32),
            pltpu.VMEM((ext, chan), f32),
        ],
        w_in.pieces + w_out.pieces,
        flops=8 * rows * width * chan,
    )


def add_rows(values, own, received):
    def body(*refs):
        total = refs[0][...]
        for ref in refs[1:-1]:
            total = total + ref[...].astype(f32)
        refs[-1][...] = total.astype(bf16)

    return call(body, [(own.shape, bf16)], [values, own, *received])[0]


def widen(own, received, nz):
    share, width = own.shape

    def body(*refs):
        join_rows(refs[-1], refs[:-1], lax.axis_index("tensor"))

    return call(body, [((share * nz, width), f32)], [own, *received])[0]


def part(value, axis, count, index):
    size = value.shape[axis] // count
    return lax.dynamic_slice_in_dim(value, index * size, size, axis)


def fold(value, axis, count, index, name, scale):
    total = part(value, axis, count, index).astype(f32)
    for mask in range(1, count):
        piece = part(value, axis, count, index ^ mask).astype(bf16)
        total = total + swap(piece, name, mask * scale).astype(f32)
    return total


def spread(piece, axis, count, index, name, scale):
    shape = list(piece.shape)
    shape[axis] *= count
    full = jnp.zeros(shape, piece.dtype)
    size = piece.shape[axis]
    full = lax.dynamic_update_slice_in_dim(full, piece, index * size, axis)
    for mask in range(1, count):
        full = lax.dynamic_update_slice_in_dim(
            full, swap(piece, name, mask * scale), (index ^ mask) * size, axis
        )
    return full


class Reduction:
    def __init__(self, partial, dim, cut):
        self.fs, ctx = lax.axis_index("fsdp"), lax.axis_index("context")
        self.n_fs, self.n_rest = lax.axis_size("fsdp"), lax.axis_size("context") // 2
        self.core, self.rest = ctx % 2, ctx // 2
        self.dim, self.cut, self.value = dim, cut, partial

    def over_cores(self):
        dim = self.dim
        if dim == self.cut:
            shape = self.value.shape
            self.size = shape[dim] // self.n_fs
            wide = self.value.reshape(shape[:dim] + (self.n_fs, self.size) + shape[dim + 1 :])
            self.value = fold(wide, dim + 1, 2, self.core, "context", 1)
        else:
            self.value = fold(self.value, self.cut, 2, self.core, "context", 1)

    def over_fsdp(self):
        dim = self.dim
        self.value = fold(self.value, dim, self.n_fs, self.fs, "fsdp", 1)
        if dim == self.cut:
            shape = self.value.shape
            self.value = self.value.reshape(shape[:dim] + (shape[dim + 1],) + shape[dim + 2 :])

    def over_rest(self):
        value = fold(self.value, self.cut, self.n_rest, self.rest, "context", 2)
        self.value = value.astype(bf16)

    def spread_rest(self):
        self.value = spread(self.value, self.cut, self.n_rest, self.rest, "context", 2)

    def spread_cores(self):
        return join_cores(self.value, swap(self.value, "context", 1), self.cut)


def join_cores(own, other, cut):
    half = own.shape[cut]
    shape = tuple(2 * s if axis == cut else s for axis, s in enumerate(own.shape))

    def body(own_ref, other_ref, out_ref):
        core = lax.axis_index("context") % 2
        for ref, owner in ((own_ref, core), (other_ref, 1 - core)):
            index = [slice(None)] * len(shape)
            index[cut] = pl.ds(mult(owner * half, half), half)
            out_ref[tuple(index)] = ref[...].astype(f32)

    return call(body, [(shape, f32)], [own, other])[0]


def sum_blocks(own, received):
    terms = [own, *received]
    while len(terms) > 1:
        terms = [terms[i] + terms[i + 1] for i in range(0, len(terms), 2)]
    return terms[0]


def butterfly(value, axis):
    mask = 1
    while mask < lax.axis_size(axis):
        value = value + swap(value, axis, mask)
        mask *= 2
    return value


def local(tokens, cotangent, lengths, w_in, w_out, w_gate_up, w_down, norm_gains, conv_kernel):
    nz, n_fs = lax.axis_size("tensor"), lax.axis_size("fsdp")
    me = lax.axis_index("fsdp")
    own_tokens, cot_rows = tokens[0], cotangent[0]

    in_first = fetch_shards(w_in, 1)
    out_first = fetch_shards(w_out, 0)
    gain_others = [swap(norm_gains, "fsdp", mask) for mask in range(1, n_fs)]
    before = shifted(own_tokens[-halo:], "context", 1)
    behind = shifted(own_tokens[:halo], "context", -1)
    in_second = swap_cores(in_first)
    out_second = swap_cores(out_first)
    gain_width = norm_gains.shape[1]
    gains = lax.dynamic_update_slice_in_dim(
        jnp.zeros((2, gain_width * n_fs), bf16), norm_gains, me * gain_width, 1
    )
    for mask in range(1, n_fs):
        gains = lax.dynamic_update_slice_in_dim(
            gains, gain_others[mask - 1], (me ^ mask) * gain_width, 1
        )
    gate_up_first = fetch_shards(after(w_gate_up, *in_first, *out_first), 1)
    down_first = fetch_shards(after(w_down, *gate_up_first), 0)
    gate_up_second = swap_cores(gate_up_first)
    down_second = swap_cores(down_first)
    whole_in = Assembled([w_in, *in_first, *in_second], 1, 1, n_fs)
    whole_out = Assembled([w_out, *out_first, *out_second], 1, 0, n_fs)
    whole_gate_up = Assembled([w_gate_up, *gate_up_first, *gate_up_second], 1, 1, n_fs)
    whole_down = Assembled([w_down, *down_first, *down_second], 1, 0, n_fs)

    result = mixer_forward(
        lengths, own_tokens, before, behind, gains[0:1], conv_kernel, whole_in, whole_out, nz
    )
    parts, (hidden_one, b_ext, c_ext, x_ext, gated) = result[:nz], result[nz:]
    others = tensor_swap(parts)
    first_sum, h2_own = first_norm(parts[0], others, own_tokens, gains[1:2])
    h2_others = tensor_swap([h2_own] * nz)

    result = feed_forward(h2_own, h2_others, cot_rows, whole_gate_up, whole_down, nz)
    parts, (hidden_two, grad_gate, grad_up, act) = result[:nz], result[nz:]
    grad_h2_others = tensor_swap(parts)

    gate_up = Reduction(
        jnp.stack([dot_left(hidden_two, grad_gate), dot_left(hidden_two, grad_up)]), 1, 1
    )
    down = Reduction(dot_left(act, cot_rows), 1, 0)
    gate_up.over_cores()
    down.over_cores()
    down_parts = down_product(act, whole_down, nz)

    grad_first, grad_first_b, grad_gain_two = norm_back(
        parts[0], grad_h2_others, first_sum, gains[1:2], cot_rows
    )
    grad_first_others = tensor_swap([grad_first_b] * nz)
    ahead = shifted(grad_first_b[:halo], "context", -1)
    aheads = [ahead, *tensor_swap([ahead] * nz)]

    down.over_fsdp()
    gate_up.over_fsdp()
    down_others = tensor_swap(down_parts)

    result = mixer_backward(
        lengths,
        grad_first_b,
        grad_first_others,
        aheads,
        b_ext,
        c_ext,
        x_ext,
        conv_kernel,
        whole_in,
        whole_out,
        nz,
    )
    parts, (grad_first_whole, grad_b, grad_c, grad_x, grad_taps) = result[:nz], result[nz:]
    grad_h1_others = tensor_swap(parts)
    out = Reduction(dot_left(gated, grad_first_whole), 1, 0)
    inp = Reduction(
        jnp.stack(
            [
                dot_left(hidden_one, grad_b),
                dot_left(hidden_one, grad_c),
                dot_left(hidden_one, grad_x),
            ]
        ),
        1,
        1,
    )
    out.over_cores()
    inp.over_cores()
    _, grad_tokens_b, grad_gain_one = norm_back(
        parts[0], grad_h1_others, own_tokens, gains[0:1], grad_first
    )
    grad_tokens_others = tensor_swap([grad_tokens_b] * nz)
    rows_out = add_rows(first_sum, down_parts[0], down_others)
    output_others = tensor_swap([rows_out] * nz)

    down.over_rest()
    down.spread_rest()
    gate_up.over_rest()
    gate_up.spread_rest()
    out.over_fsdp()
    inp.over_fsdp()
    out.over_rest()
    out.spread_rest()
    inp.over_rest()
    inp.spread_rest()
    down_total = down.spread_cores()
    gate_up_total = gate_up.spread_cores()
    out_total = out.spread_cores()
    in_total = inp.spread_cores()

    small = jnp.concatenate([grad_gain_one, grad_gain_two], axis=0)
    small = sum_blocks(small, tensor_swap([small] * nz))
    n_gain = small.size
    small = jnp.concatenate([small.reshape(-1), grad_taps.reshape(-1)])
    small = butterfly(butterfly(small, "context"), "fsdp")
    gains_total = lax.dynamic_slice_in_dim(
        small[:n_gain].reshape(2, -1), me * gain_width, gain_width, 1
    )
    kernel_total = small[n_gain:].reshape(grad_taps.shape)

    return (
        widen(rows_out, output_others, nz)[None],
        widen(grad_tokens_b, grad_tokens_others, nz)[None],
        in_total,
        out_total,
        gate_up_total,
        down_total,
        gains_total,
        kernel_total,
    )


def solution(mesh):
    placed = (
        P("fsdp", "context", None),
        P("fsdp", "context", None),
        P("fsdp", None),
        P(None, "fsdp", "tensor"),
        P("tensor", "fsdp"),
        P(None, "fsdp", "tensor"),
        P("tensor", "fsdp"),
        P(None, "fsdp"),
        P(None, "tensor"),
    )
    return jax.shard_map(
        lambda *args: local(*args),
        mesh=mesh,
        in_specs=placed,
        out_specs=(
            P("fsdp", "context", None),
            P("fsdp", "context", None),
            P(None, "fsdp", "tensor"),
            P("tensor", "fsdp"),
            P(None, "fsdp", "tensor"),
            P("tensor", "fsdp"),
            P(None, "fsdp"),
            P(None, "tensor"),
        ),
        check_vma=False,
    )
```
